512 devices in a mesh: vocab: 64 (over y, z_hi, core), width: 8 (over z_lo, x).
Axes of the slice: x: 4, y: 8, z: 8 (z_hi: 4, z_lo: 2; z = z_hi * 2 + z_lo), core: 2. Of those that a mesh axis runs over, the one named last changes fastest.
Arguments:
- head_weight: bfloat16 [4096, 65536], P('width', 'vocab'), may hold values from -3 to 3
- direction: bfloat16 [4096, 65536], P('width', 'vocab'), may hold values from -150 to 150
- residual: bfloat16 [4096, 65536], P('width', 'vocab'), may hold values from -150 to 150
- hidden: bfloat16 [512, 4096], P('vocab', 'width'), may hold values from -200 to 200
- fold_ids: int32 [512], replicated, may hold values from 0 to 7
Outputs:
- new_direction: bfloat16 [4096, 65536], P('width', 'vocab')
The draws below stay inside these ranges and needn't reach their ends.
All inputs are finite; a program needn't handle non-finite values.
Results may differ from the reference program's by a relative error of at most 0.0085.
Values may be sent and summed in bfloat16 or wider, within the bound.
A program may use at most 64 MiB of HBM per device.

```python
import math
import jax
import jax.numpy as jnp
from jax import lax

D = 4096
VOCAB_DEV = 1024
TOK_DEV = 8
FOLDS = 8
VOCAB = 65536
TOKENS = 512
N_VOCAB = 64


def log_scales(key, count, lowest, highest):
    return jnp.exp(jax.random.uniform(key, (count,), jnp.float32, math.log(lowest), math.log(highest)))


def hidden_base():
    return math.sqrt(0.004 * VOCAB_DEV / TOK_DEV)


def head_spread():
    return 0.125 / (hidden_base() * math.sqrt(D))


def head_field(key):
    own_key = jax.random.fold_in(key, 7)
    col_key, value_key, pair_key = jax.random.split(own_key, 3)
    col_scale = log_scales(col_key, VOCAB, 0.5, 5.0)
    spread = head_spread()
    leads = 2 * jax.random.permutation(pair_key, VOCAB // 2)[:6]
    col_scale = col_scale.at[leads].set(5.0).at[leads + 1].set(5.0)
    values = jnp.clip(jax.random.normal(value_key, (D, VOCAB), jnp.float32), -6.0, 6.0)
    weight = spread * values * col_scale[None, :]
    return weight


def scaled_field(key, salt):
    own_key = jax.random.fold_in(key, salt)
    row_key, col_key, value_key = jax.random.split(own_key, 3)
    row_ramp = (1.0 + 2.0 * jnp.arange(D, dtype=jnp.float32) / D) / 2.0
    col_ramp = (1.0 + 2.0 * jnp.arange(VOCAB, dtype=jnp.float32) / VOCAB) / 2.0
    row_scale = log_scales(row_key, D, 0.3, 3.0) * row_ramp
    col_scale = log_scales(col_key, VOCAB, 0.3, 3.0) * col_ramp
    values = jnp.clip(jax.random.normal(value_key, (D, VOCAB), jnp.float32), -6.0, 6.0)
    return values * row_scale[:, None] * col_scale[None, :]


def draw_head_weight(key, part):
    weight = head_field(key)
    return weight.astype(jnp.bfloat16)


def draw_direction(key, part):
    return scaled_field(key, 21).astype(jnp.bfloat16)


def draw_residual(key, part):
    return scaled_field(key, 33).astype(jnp.bfloat16)


def draw_hidden(key, part):
    own_key = jax.random.fold_in(key, 11)
    row_key, value_key = jax.random.split(own_key, 2)
    row_scale = log_scales(row_key, TOKENS, 0.4, 4.0) * hidden_base()
    values = jnp.clip(jax.random.normal(value_key, (TOKENS, D), jnp.float32), -6.0, 6.0)
    field = values * row_scale[:, None]
    return field.astype(jnp.bfloat16)


def place_ends(drawn, key, smallest, top_value):
    place = [jax.random.randint(jax.random.fold_in(key, axis), (), 0, length) for axis, length in enumerate(drawn.shape)]
    widest = drawn.shape.index(max(drawn.shape))
    beside = place[:widest] + [(place[widest] + 1) % drawn.shape[widest]] + place[widest + 1:]
    return drawn.at[tuple(place)].set(smallest).at[tuple(beside)].set(top_value)


def setup_inputs(seed: int = 0) -> dict:
    streams_of = jax.random.split(jax.random.key(seed), 6)
    head_weight = draw_head_weight(jax.random.fold_in(streams_of[5], 71), 0)
    direction = draw_direction(jax.random.fold_in(streams_of[5], 71), 0)
    residual = draw_residual(jax.random.fold_in(streams_of[5], 71), 0)
    hidden = draw_hidden(jax.random.fold_in(streams_of[5], 71), 0)
    fold_ids = place_ends(jax.random.randint(streams_of[4], (TOKENS,), 0, FOLDS), jax.random.fold_in(streams_of[4], 1), 0, FOLDS - 1).astype(jnp.int32)
    return {"head_weight": head_weight, "direction": direction, "residual": residual, "hidden": hidden, "fold_ids": fold_ids}


DAMPING = 0.02


def reference(head_weight, direction, residual, hidden, fold_ids):
    logits = jnp.dot(hidden, head_weight, preferred_element_type=jnp.float32)
    tangent = jnp.dot(hidden, direction, preferred_element_type=jnp.float32)
    row_top = jnp.max(logits, axis=1, keepdims=True)
    weights = jnp.exp(logits - row_top)
    row_total = jnp.sum(weights, axis=1, keepdims=True)
    row_moment = jnp.sum(weights * tangent, axis=1, keepdims=True)
    kept_mask = (fold_ids != 0).astype(jnp.float32)[:, None]
    curving = (kept_mask * (weights / row_total) * (tangent - row_moment / row_total)).astype(jnp.bfloat16)
    block_ids = jnp.arange(N_VOCAB, dtype=jnp.int32)

    def image_block(block_index):
        offset = (block_index * VOCAB_DEV).astype(jnp.int32)
        curve_block = lax.dynamic_slice_in_dim(curving, offset, VOCAB_DEV, 1)
        direction_block = lax.dynamic_slice_in_dim(direction, offset, VOCAB_DEV, 1).astype(jnp.float32)
        residual_block = lax.dynamic_slice_in_dim(residual, offset, VOCAB_DEV, 1).astype(jnp.float32)
        product = jnp.dot(hidden.T, curve_block, preferred_element_type=jnp.float32)
        return product + DAMPING * direction_block, direction_block, residual_block

    def first_pass(carry, block_index):
        operator_image, direction_block, residual_block = image_block(block_index)
        squares = carry[0] + jnp.sum(residual_block * residual_block)
        curvature_sum = carry[1] + jnp.sum(direction_block * operator_image)
        return (squares, curvature_sum), None

    start_sums = (jnp.zeros((), jnp.float32), jnp.zeros((), jnp.float32))
    (squares, curvature_sum), _ = lax.scan(first_pass, start_sums, block_ids)
    step_size = squares / curvature_sum

    def second_pass(block_index):
        operator_image, direction_block, residual_block = image_block(block_index)
        return residual_block - step_size * operator_image

    moved_blocks = lax.map(second_pass, block_ids)
    next_squares = jnp.sum(moved_blocks * moved_blocks)
    mixing = next_squares / squares
    moved = jnp.transpose(moved_blocks, (1, 0, 2)).reshape(D, VOCAB)
    return (moved + mixing * direction.astype(jnp.float32)).astype(jnp.bfloat16)
```

```python
import jax
import jax.numpy as jnp
from jax import lax
from jax.experimental import pallas as pl
from jax.experimental.pallas import tpu as pltpu
from jax.sharding import PartitionSpec as P

DAMPING = 0.02
MESH = pl.DeviceIdType.MESH
NY, NZH, NC, NZL, NX = 8, 4, 2, 2, 4
F = 512
CW = 256


def kernel(
    head, dirn, res, hid, fold, out,
    hg, wb, dv, rv, img, cb, hown, ht, hsib, hblk, own, zs, zr,
    a1, a2, a3, b1, b2, b3,
    sib_s, sib_r, hx_s, hx_r, hz_s, hz_r, yr_s, yr_r, sb_s, sb_r,
    w_s, w_r, loc, z_s, z_r, cz_s, cz_r, cx_s, cx_r,
    a1_s, a1_r, a2_s, a2_r, a3_s, a3_r,
    b1_s, b1_r, b2_s, b2_r, b3_s, b3_r,
):
    f32, bf16 = jnp.float32, jnp.bfloat16
    hf = F // 2
    hl = NX * hf
    ch = CW // 2
    nb = NY * NZH
    nb2 = nb // 2
    tok = 16 * nb
    th = tok // 2
    right_steps, left_steps = NY // 2, (NY - 1) // 2

    v = lax.axis_index("vocab")
    w = lax.axis_index("width")
    c = lax.rem(v, NC)
    zh = lax.rem(lax.div(v, NC), NZH)
    y = lax.div(v, NC * NZH)
    x = lax.rem(w, NX)
    zl = lax.div(w, NX)
    yz = y * NZH + zh

    def dev(dy=0, dzh=0, dc=0, dzl=0, dx=0):
        yy = lax.rem(y + dy, NY)
        zz = lax.rem(zh + dzh, NZH)
        cc_ = lax.rem(c + dc, NC)
        ll = lax.rem(zl + dzl, NZL)
        xx = lax.rem(x + dx, NX)
        return ((yy * NZH + zz) * NC + cc_, ll * NX + xx)

    peers = []
    for dl in range(NZL):
        for dx in range(NX):
            for dc in range(NC):
                if dl or dx or dc:
                    peers.append(dict(dzl=dl, dx=dx, dc=dc))
    for d in range(1, NY):
        peers.append(dict(dy=d))
    for d in range(1, NZH):
        peers.append(dict(dzh=d))

    sends = []

    def push(src, dst, ssem, rsem, **where):
        d = pltpu.make_async_remote_copy(
            src_ref=src, dst_ref=dst, send_sem=ssem, recv_sem=rsem,
            device_id=dev(**where), device_id_type=MESH,
        )
        d.start()
        sends.append(d)

    def got(dst, rsem):
        pltpu.make_async_copy(dst, dst, rsem).wait()

    barrier = pltpu.get_barrier_semaphore()
    for p in peers:
        pl.semaphore_signal(barrier, inc=1, device_id=dev(**p), device_id_type=MESH)
    pl.semaphore_wait(barrier, len(peers))

    push(hid.at[:, pl.ds(pl.multiple_of((1 - c) * hf, 128), hf)], hsib, sib_s, sib_r, dc=1)
    locals_ = []

    def bring(src, dst, sem):
        d = pltpu.make_async_copy(src, dst, sem)
        d.start()
        locals_.append(d)
        return d

    mine_copy = pltpu.make_async_copy(
        hid.at[:, pl.ds(pl.multiple_of(c * hf, 128), hf)], hblk.at[0], loc.at[0]
    )
    mine_copy.start()
    mine_copy.wait()
    got(hsib, sib_r)
    mine = hblk[0].astype(f32)
    other = hsib[...].astype(f32)
    first = c == 0
    lo = jnp.where(first, mine, other)
    hi = jnp.where(first, other, mine)
    hown[0, :, 0:hf] = jnp.concatenate([lo, hi], axis=0).astype(bf16)
    block = hown.at[0, :, pl.ds(0, hf)]

    def spot(xx):
        return hg.at[yz, :, pl.ds(pl.multiple_of(c * hl + xx * hf, 128), hf)]

    for dx in range(1, NX):
        push(block, spot(x), hx_s.at[dx], hx_r.at[dx], dx=dx)
    spot_copy = pltpu.make_async_copy(block, spot(x), loc.at[1])
    spot_copy.start()

    arrays = (head, dirn)
    order = [(1, 0), (0, 0), (1, 1), (0, 1)]
    own_w = {}
    for arr, cc in order:
        for dx in range(1, NX):
            xx = lax.rem(x + dx, NX)
            push(
                arrays[arr].at[:, :, pl.ds(pl.multiple_of(xx * CW + cc * ch, 128), ch)],
                wb.at[arr, cc, :, x], w_s.at[arr, cc, dx], w_r.at[arr, cc, dx], dx=dx,
            )
        own_w[arr, cc] = pltpu.make_async_copy(
            arrays[arr].at[:, :, pl.ds(pl.multiple_of(x * CW + cc * ch, 128), ch)],
            wb.at[arr, cc, :, x], loc.at[2 + arr * 2 + cc],
        )
        own_w[arr, cc].start()
    keeps = []
    for xb in range(NX):
        for k, (src, dst) in enumerate(((dirn, dv), (res, rv))):
            d = pltpu.make_async_copy(
                src.at[:, :, pl.ds(xb * CW, CW)], dst.at[xb], loc.at[6 + 2 * xb + k]
            )
            d.start()
            keeps.append(d)

    spot_copy.wait()
    for dx in range(1, NX):
        got(spot(lax.rem(x + NX - dx, NX)), hx_r.at[dx])

    def slot(yy, zz, cc_):
        return hg.at[yy * NZH + zz, :, pl.ds(pl.multiple_of(cc_ * hl, 128), hl)]

    mine_slot = slot(y, zh, c)
    for d in range(1, NZH):
        push(mine_slot, mine_slot, hz_s.at[d], hz_r.at[d], dzh=d)

    def relay(ref, k, j):
        push(ref, ref, sb_s.at[k, j], sb_r.at[k, j], dc=1)

    for j in range(NZH):
        zz = lax.rem(zh + NZH - j, NZH)
        ref = slot(y, zz, c)
        if j:
            got(ref, hz_r.at[j])
        if right_steps:
            push(ref, ref, yr_s.at[0, 0, j], yr_r.at[0, 0, j], dy=1)
        if left_steps:
            push(ref, ref, yr_s.at[1, 0, j], yr_r.at[1, 0, j], dy=NY - 1)
        relay(ref, 0, j)
    ring = [(0, 0)]
    for s in range(1, right_steps + 1):
        for j in range(NZH):
            zz = lax.rem(zh + NZH - j, NZH)
            ref = slot(lax.rem(y + NY - s, NY), zz, c)
            got(ref, yr_r.at[0, s - 1, j])
            if s < right_steps:
                push(ref, ref, yr_s.at[0, s, j], yr_r.at[0, s, j], dy=1)
            relay(ref, s, j)
            if s <= left_steps:
                ref = slot(lax.rem(y + s, NY), zz, c)
                got(ref, yr_r.at[1, s - 1, j])
                if s < left_steps:
                    push(ref, ref, yr_s.at[1, s, j], yr_r.at[1, s, j], dy=NY - 1)
                relay(ref, right_steps + s, j)
    for j in range(NZH):
        zz = lax.rem(zh + NZH - j, NZH)
        for s in range(right_steps + 1):
            got(slot(lax.rem(y + NY - s, NY), zz, 1 - c), sb_r.at[s, j])
        for s in range(1, left_steps + 1):
            got(slot(lax.rem(y + s, NY), zz, 1 - c), sb_r.at[right_steps + s, j])

    for arr, cc in order:
        for dx in range(1, NX):
            got(wb.at[arr, cc, :, lax.rem(x + NX - dx, NX)], w_r.at[arr, cc, dx])
        own_w[arr, cc].wait()
        wm = wb[arr, cc].reshape(2 * hl, ch)
        hp = hg[pl.ds((1 - zl) * nb2, nb2)].reshape(th, 2 * hl)
        zs[arr, cc] = jnp.dot(hp, wm, preferred_element_type=f32)
        push(zs.at[arr, cc], zr.at[arr, cc], z_s.at[arr, cc], z_r.at[arr, cc], dzl=1)
        ho = hg[pl.ds(zl * nb2, nb2)].reshape(th, 2 * hl)
        own[arr, cc] = jnp.dot(ho, wm, preferred_element_type=f32)

    tails = []
    for h in range(2):
        d = pltpu.make_async_copy(
            hg.at[:, :, pl.ds(pl.multiple_of(h * hl + x * hf, 128), hf)],
            hown.at[:, :, pl.ds(h * hf, hf)], loc.at[6 + 2 * NX + h],
        )
        tails.append(d)
    for dx in range(1, NX):
        sends[dx].wait_send()
    for d in tails:
        d.start()

    for arr, cc in order:
        got(zr.at[arr, cc], z_r.at[arr, cc])
    for cc in range(2):
        for arr in range(2):
            own[arr, cc] = own[arr, cc] + zr[arr, cc]
    top = jnp.maximum(
        jnp.max(own[0, 0], axis=1, keepdims=True), jnp.max(own[0, 1], axis=1, keepdims=True)
    )
    total = jnp.zeros((th, 1), f32)
    moment = jnp.zeros((th, 1), f32)
    for cc in range(2):
        e = jnp.exp(own[0, cc] - top)
        own[0, cc] = e
        total = total + jnp.sum(e, axis=1, keepdims=True)
        moment = moment + jnp.sum(e * own[1, cc], axis=1, keepdims=True)
    lane = lax.broadcasted_iota(jnp.int32, (th, 128), 1)
    packed = jnp.where(lane == 0, top, jnp.where(lane == 1, total, moment))
    a1[0] = jnp.transpose(packed)[0:4]

    def merge(ref, n):
        tops = [ref[k, 0:1, :] for k in range(n)]
        m = tops[0]
        for t in tops[1:]:
            m = jnp.maximum(m, t)
        s = jnp.zeros_like(m)
        q = jnp.zeros_like(m)
        for k in range(n):
            g = jnp.exp(tops[k] - m)
            s = s + g * ref[k, 1:2, :]
            q = q + g * ref[k, 2:3, :]
        return m, s, q

    def put(ref, rows):
        for i, r in enumerate(rows):
            ref[0, i:i + 1, :] = r

    stage1 = [(dx, dc) for dx in range(NX) for dc in range(NC) if dx or dc]
    for dx, dc in stage1:
        k = dx * NC + dc
        push(a1.at[0], a1.at[k], a1_s.at[k], a1_r.at[k], dx=dx, dc=dc)
    for d in tails:
        d.wait()
    ht[...] = jnp.transpose(hown[...].reshape(tok, F).astype(f32)).astype(bf16)
    for dx, dc in stage1:
        k = dx * NC + dc
        got(a1.at[k], a1_r.at[k])
    put(a2, merge(a1, NX * NC))
    for d in range(1, NY):
        push(a2.at[0], a2.at[d], a2_s.at[d], a2_r.at[d], dy=d)
    for d in range(1, NY):
        got(a2.at[d], a2_r.at[d])
    put(a3, merge(a2, NY))
    for d in range(1, NZH):
        push(a3.at[0], a3.at[d], a3_s.at[d], a3_r.at[d], dzh=d)
    for d in range(1, NZH):
        got(a3.at[d], a3_r.at[d])
    m, s, q = merge(a3, NZH)
    folds = jnp.where(zl == 0, fold[:, 0:th], fold[:, th:2 * th])
    keep = (folds != 0).astype(f32)
    row = lax.broadcasted_iota(jnp.int32, (128, th), 0)
    back = jnp.transpose(jnp.where(row == 0, m, jnp.where(row == 1, keep / s, q / s)))
    factor = jnp.exp(top - back[:, 0:1]) * back[:, 1:2]
    mean = back[:, 2:3]
    for cc in range(2):
        cb[x, zl, :, cc * ch:(cc + 1) * ch] = (
            own[0, cc] * factor * (own[1, cc] - mean)
        ).astype(bf16)

    ol = 1 - zl
    xl, xr, xo = lax.rem(x + NX - 1, NX), lax.rem(x + 1, NX), lax.rem(x + 2, NX)

    def cpush(ref, i, **where):
        push(ref, ref, cx_s.at[i], cx_r.at[i], **where)

    me = cb.at[x, zl]
    push(me, me, cz_s, cz_r, dzl=1)
    if NX == 4:
        cpush(me, 0, dx=1)
        cpush(me, 1, dx=NX - 1)
    got(cb.at[x, ol], cz_r)
    if NX == 4:
        cpush(cb.at[x, ol], 2, dx=1)
        cpush(cb.at[x, ol], 3, dx=NX - 1)
        got(cb.at[xl, zl], cx_r.at[0])
        cpush(cb.at[xl, zl], 4, dx=1)

    for d in keeps:
        d.wait()

    sums = [jnp.zeros((1, CW), f32) for _ in range(4)]

    def image(xb, sums):
        block = jnp.dot(ht[...], cb[xb].reshape(tok, CW), preferred_element_type=f32)
        d = dv[xb].reshape(F, CW).astype(f32)
        r = rv[xb].reshape(F, CW).astype(f32)
        g = block + DAMPING * d
        img[xb] = g
        terms = (r * r, r * g, g * g, d * g)
        return [a + jnp.sum(t, axis=0, keepdims=True) for a, t in zip(sums, terms)]

    sums = image(x, sums)
    if NX == 4:
        got(cb.at[xr, ol], cx_r.at[3])
        cpush(cb.at[xr, ol], 5, dx=NX - 1)
        got(cb.at[xr, zl], cx_r.at[1])
        sums = image(xr, sums)
        got(cb.at[xl, ol], cx_r.at[2])
        sums = image(xl, sums)
        got(cb.at[xo, zl], cx_r.at[4])
        got(cb.at[xo, ol], cx_r.at[5])
        sums = image(xo, sums)

    put(b1, sums)
    stage1 = [
        (dl, dx, dc) for dl in range(NZL) for dx in range(NX) for dc in range(NC)
        if dl or dx or dc
    ]
    for dl, dx, dc in stage1:
        k = (dl * NX + dx) * NC + dc
        push(b1.at[0], b1.at[k], b1_s.at[k], b1_r.at[k], dx=dx, dc=dc, dzl=dl)
    for dl, dx, dc in stage1:
        k = (dl * NX + dx) * NC + dc
        got(b1.at[k], b1_r.at[k])

    def add(ref, n):
        s = ref[0]
        for k in range(1, n):
            s = s + ref[k]
        return s

    b2[0] = add(b1, NZL * NX * NC)
    for d in range(1, NY):
        push(b2.at[0], b2.at[d], b2_s.at[d], b2_r.at[d], dy=d)
    for d in range(1, NY):
        got(b2.at[d], b2_r.at[d])
    b3[0] = add(b2, NY)
    for d in range(1, NZH):
        push(b3.at[0], b3.at[d], b3_s.at[d], b3_r.at[d], dzh=d)
    for d in range(1, NZH):
        got(b3.at[d], b3_r.at[d])
    sums = jnp.sum(add(b3, NZH), axis=1, keepdims=True)
    rr, ri, ii, di = sums[0:1], sums[1:2], sums[2:3], sums[3:4]
    step = rr / di
    mixing = (rr + step * (step * ii - 2.0 * ri)) / rr
    for xb in range(NX):
        d = dv[xb].reshape(F, CW).astype(f32)
        r = rv[xb].reshape(F, CW).astype(f32)
        out[:, xb * CW:(xb + 1) * CW] = ((r - step * img[xb]) + mixing * d).astype(bf16)

    for i, d in enumerate(sends):
        if not 1 <= i < NX:
            d.wait_send()


def local(head_weight, direction, residual, hidden, fold_ids):
    f32, bf16 = jnp.float32, jnp.bfloat16
    hf, ch = F // 2, CW // 2
    nb = NY * NZH
    tok = 16 * nb
    th = tok // 2
    vd = NX * CW
    vm, dma = pltpu.VMEM, pltpu.SemaphoreType.DMA
    anyspace = pl.BlockSpec(memory_space=pl.ANY)
    vspace = pl.BlockSpec(memory_space=pltpu.VMEM)

    def pair(*shape):
        return [dma(shape) if shape else dma, dma(shape) if shape else dma]

    scratch = [
        vm((nb, 16, 2 * NX * hf), bf16),
        vm((2, 2, 2, NX, hf, ch), bf16),
        vm((NX, 2, hf, CW), bf16),
        vm((NX, 2, hf, CW), bf16),
        vm((NX, F, CW), f32),
        vm((NX, NZL, th, CW), bf16),
        vm((nb, 16, F), bf16),
        vm((F, tok), bf16),
        vm((8, hf), bf16),
        vm((1, 8, hf), bf16),
        vm((2, 2, th, ch), f32),
        vm((2, 2, th, ch), f32),
        vm((2, 2, th, ch), f32),
        vm((NX * NC, 4, th), f32),
        vm((NY, 4, th), f32),
        vm((NZH, 4, th), f32),
        vm((NZL * NX * NC, 4, CW), f32),
        vm((NY, 4, CW), f32),
        vm((NZH, 4, CW), f32),
        *pair(), *pair(NX), *pair(NZH), *pair(2, max(NY // 2, 1), NZH), *pair(NY, NZH),
        *pair(2, 2, NX), dma((8 + 2 * NX,)), *pair(2, 2), *pair(), *pair(6),
        *pair(NX * NC), *pair(NY), *pair(NZH),
        *pair(NZL * NX * NC), *pair(NY), *pair(NZH),
    ]
    return pl.pallas_call(
        kernel,
        out_shape=jax.ShapeDtypeStruct((F, vd), bf16),
        in_specs=[anyspace, anyspace, anyspace, vspace, vspace],
        out_specs=vspace,
        scratch_shapes=scratch,
        compiler_params=pltpu.CompilerParams(
            collective_id=0, has_side_effects=True, vmem_limit_bytes=48 * 1024 * 1024
        ),
    )(
        head_weight.reshape(2, hf, vd), direction.reshape(2, hf, vd),
        residual.reshape(2, hf, vd), hidden, fold_ids.reshape(1, tok),
    )


def solution(mesh):
    placed = (
        P("width", "vocab"),
        P("width", "vocab"),
        P("width", "vocab"),
        P("vocab", "width"),
        P(),
    )
    return jax.shard_map(
        local, mesh=mesh, in_specs=placed, out_specs=P("width", "vocab"), check_vma=False
    )
```

```python
import jax
import jax.numpy as jnp
from jax import lax
from jax.experimental import pallas as pl
from jax.experimental.pallas import tpu as pltpu
from jax.sharding import PartitionSpec as P

DAMPING = 0.02
MESH = pl.DeviceIdType.MESH
NY, NZH, NC, NZL, NX = 8, 4, 2, 2, 4
F = 512
CW = 256


def kernel(
    head, dirn, res, hid, fold_hbm, img_out, scal,
    fold, hp, hz, hq, hg, wb, dv, rv, img, cb, hown, ht, own, zs, zr, us, ur,
    a1, a2, a3, b1, b2, b3,
    hx_s, hx_r, hz_s, hz_r, yr_s, yr_r, sb_s, sb_r,
    w_s, w_r, loc, z_s, z_r, u_s, u_r, cz_s, cz_r, cx_s, cx_r,
    a1_s, a1_r, a2_s, a2_r, a3_s, a3_r,
    b1_s, b1_r, b2_s, b2_r, b3_s, b3_r,
):
    f32, bf16 = jnp.float32, jnp.bfloat16
    hf = F // 2
    hl = NX * hf
    nb = NY * NZH
    nb2 = nb // 2
    tok = 16 * nb
    th = tok // 2
    qt = th // 2
    nz = NZH * NZL

    v = lax.axis_index("vocab")
    w = lax.axis_index("width")
    c = lax.rem(v, NC)
    zh = lax.rem(lax.div(v, NC), NZH)
    y = lax.div(v, NC * NZH)
    x = lax.rem(w, NX)
    zl = lax.div(w, NX)
    z = zh * NZL + zl

    xs = [x] + [lax.rem(x + d, NX) for d in range(1, NX)]
    ys = [y] + [lax.rem(y + d, NY) for d in range(1, NY)]
    hs = [zh] + [lax.rem(zh + d, NZH) for d in range(1, NZH)]
    cs = [c, 1 - c]
    ls = [zl, 1 - zl]
    zs_ = [z] + [lax.rem(z + d, nz) for d in range(1, nz)]
    vy = [i * (NZH * NC) for i in ys]
    vh = [i * NC for i in hs]
    wl = [i * NX for i in ls]

    def dev(dy=0, dzh=0, dc=0, dzl=0, dx=0, dz=0):
        if dz:
            hh = lax.div(zs_[dz], NZL)
            return (vy[dy] + hh * NC + cs[dc], (zs_[dz] - hh * NZL) * NX + xs[dx])
        return (vy[dy] + vh[dzh] + cs[dc], wl[dzl] + xs[dx])

    near = [(dx, dc) for dx in range(NX) for dc in range(NC) if dx or dc]
    peers = [dict(dx=dx, dc=dc) for dx, dc in near]
    peers += [dict(dy=d) for d in sorted({1, NY - 1})]
    peers += [dict(dzh=d) for d in range(1, NZH)]
    peers += [dict(dzl=1)]

    sends = []

    def push(src, dst, ssem, rsem, **where):
        d = pltpu.make_async_remote_copy(
            src_ref=src, dst_ref=dst, send_sem=ssem, recv_sem=rsem,
            device_id=dev(**where), device_id_type=MESH,
        )
        d.start()
        sends.append(d)

    def got(dst, rsem):
        pltpu.make_async_copy(dst, dst, rsem).wait()

    def bring(src, dst, i):
        d = pltpu.make_async_copy(src, dst, loc.at[i])
        d.start()
        return d

    barrier = pltpu.get_barrier_semaphore()
    for p in peers:
        pl.semaphore_signal(barrier, inc=1, device_id=dev(**p), device_id_type=MESH)
    own_piece = bring(hid.at[:, pl.ds(pl.multiple_of(c * hf, 128), hf)], hp.at[x, c, 0], 0)
    keeps = [bring(fold_hbm, fold, 1)]
    for xb in range(NX):
        keeps.append(bring(dirn.at[:, :, pl.ds(xb * CW, CW)], dv.at[xb], 2 + 2 * xb))
        keeps.append(bring(res.at[:, :, pl.ds(xb * CW, CW)], rv.at[xb], 3 + 2 * xb))
    own_w = {}
    arrays = (head, dirn)
    for arr in (1, 0):
        own_w[arr] = bring(
            arrays[arr].at[:, :, pl.ds(pl.multiple_of(x * CW, 128), CW)],
            wb.at[arr, :, x], 2 + 2 * NX + arr,
        )
    pl.semaphore_wait(barrier, len(peers))

    parts = [pl.multiple_of(i * hf, 128) for i in cs]
    for dx, dc in near:
        k = dx * NC + dc
        push(
            hid.at[:, pl.ds(parts[dc], hf)], hp.at[x, c, 0],
            hx_s.at[0, k], hx_r.at[0, k], dx=dx, dc=dc,
        )
    for d in range(1, NZH):
        push(hid, hz.at[d], hz_s.at[d], hz_r.at[d], dzh=d)

    def columns(arr, h):
        for dx in (1, 3, 2)[:NX - 1]:
            cols = pl.ds(pl.multiple_of(xs[dx] * CW, 128), CW)
            push(
                arrays[arr].at[h, :, cols], wb.at[arr, h, x],
                w_s.at[arr, h, dx], w_r.at[arr, h, dx], dx=dx,
            )

    columns(1, 0)
    own_piece.wait()

    def slot(yy, zz, cc):
        return hg.at[yy * NZH + zz, :, pl.ds(pl.multiple_of(cc * hl, 128), hl)]

    def at(k, j, cc):
        return slot(ys[-k % NY], hs[-j % NZH], cc)

    def collect(first, n):
        for dx, dc in near:
            got(
                hp.at[xs[-dx % NX], cs[dc], pl.ds(first, n)],
                hx_r.at[min(first, 1), dx * NC + dc],
            )
        for j in range(first, first + n):
            for xb in range(NX):
                hq[j, :, xb * hf:(xb + 1) * hf] = jnp.concatenate(
                    [hp[xb, 0, j].astype(f32), hp[xb, 1, j].astype(f32)], axis=0
                ).astype(bf16)
            keeps.append(bring(hq.at[j], at(0, j, c), 7 + 3 * NX + j))

    last = {(0, j): NY // 2 - (0 if 2 * j <= NZH - 1 else 1) for j in range(NZH)}
    last.update({(1, j): NY - 1 - last[0, j] for j in range(NZH)})
    free = [0.0, 0.0]
    events = []

    def ring(src, k, j, way, s, now):
        if s < last[way, j]:
            dst = at(k, j, c)
            push(src, dst, yr_s.at[way, s, j], yr_r.at[way, s, j], dy=(1, NY - 1)[way])
            begin = max(now, free[way])
            free[way] = begin + 0.8
            events.append((begin + 2.4, len(events), way, s + 1, j))

    def arrive(src, k, j, ways, s, now):
        for way in ways:
            ring(src, k, j, way, s, now)
        push(src, at(k, j, c), sb_s.at[k, j], sb_r.at[k, j], dc=1)

    collect(0, 1)
    arrive(hq.at[0], 0, 0, (0, 1), 0, 0.0)
    for d in range(1, NZH):
        got(hz.at[d], hz_r.at[d])
    if NZH > 1:
        rest = pl.ds(1, NZH - 1)
        for dx, dc in near:
            k = dx * NC + dc
            push(
                hz.at[rest, :, pl.ds(parts[dc], hf)], hp.at[x, c, rest],
                hx_s.at[1, k], hx_r.at[1, k], dx=dx, dc=dc,
            )
        rest_copy = bring(hz.at[rest, :, pl.ds(parts[0], hf)], hp.at[x, c, rest], 4 + 2 * NX)
        events.append((4.5, len(events), 2, 0, 1))
    columns(1, 1)
    columns(0, 0)
    columns(0, 1)
    done = set()
    while len(done) < len(events):
        now, tag, way, s, j = min(e for e in events if e[1] not in done)
        done.add(tag)
        if way == 2:
            rest_copy.wait()
            collect(1, NZH - 1)
            for j in range(1, NZH):
                arrive(hq.at[j], 0, j, (0, 1), 0, now)
        else:
            k = s if way == 0 else NY - s
            got(at(k, j, c), yr_r.at[way, s - 1, j])
            arrive(at(k, j, c), k, j, (way,), s, now)
    for k in range(NY):
        for j in range(NZH):
            got(at(k, j, 1 - c), sb_r.at[k, j])
    for d in keeps:
        d.wait()

    for arr in (1, 0):
        for h in range(2):
            for dx in range(1, NX):
                got(wb.at[arr, h, xs[-dx % NX]], w_r.at[arr, h, dx])
        own_w[arr].wait()
        for h in range(2):
            rows = hg[pl.ds((1 - zl) * nb2 + h * (nb2 // 2), nb2 // 2)].reshape(qt, 2 * hl)
            part = jnp.dot(rows, wb[arr].reshape(2 * hl, CW), preferred_element_type=f32)
            reach = jnp.maximum(jnp.max(jnp.abs(part), axis=1, keepdims=True), 1e-30)
            steps = (part * (32767.0 / reach) + 32768.5).astype(jnp.int32) - 32768
            zs[arr, h] = steps.astype(jnp.int16)
            push(zs.at[arr, h], zr.at[arr, h], z_s.at[arr, h], z_r.at[arr, h], dzl=1)
            wide = jnp.broadcast_to(reach * (1.0 / 32767.0), (qt, 128))
            us[arr, h] = jnp.transpose(wide)[0:1]
            push(us.at[arr, h], ur.at[arr, h], u_s.at[arr, h], u_r.at[arr, h], dzl=1)
        rows = hg[pl.ds(zl * nb2, nb2)].reshape(th, 2 * hl)
        own[arr] = jnp.dot(rows, wb[arr].reshape(2 * hl, CW), preferred_element_type=f32)

    tails = [
        bring(
            hg.at[:, :, pl.ds(pl.multiple_of(h * hl + x * hf, 128), hf)],
            hown.at[:, :, pl.ds(h * hf, hf)], 5 + 2 * NX + h,
        )
        for h in range(2)
    ]
    for d in tails:
        d.wait()
    ht[...] = jnp.transpose(hown[...].reshape(tok, F).astype(f32)).astype(bf16)

    def whole(arr):
        parts = []
        for h in range(2):
            got(ur.at[arr, h], u_r.at[arr, h])
            unit = jnp.transpose(jnp.broadcast_to(ur[arr, h], (128, qt)))[:, 0:1]
            got(zr.at[arr, h], z_r.at[arr, h])
            parts.append(
                own[arr, h * qt:(h + 1) * qt] + zr[arr, h].astype(jnp.int32).astype(f32) * unit
            )
        return jnp.concatenate(parts, axis=0)

    tangent = whole(1)
    logits = whole(0)
    top = jnp.max(logits, axis=1, keepdims=True)
    e = jnp.exp(logits - top)
    total = jnp.sum(e, axis=1, keepdims=True)
    moment = jnp.sum(e * tangent, axis=1, keepdims=True)
    own[0] = e
    own[1] = tangent
    lane = lax.broadcasted_iota(jnp.int32, (th, 128), 1)
    packed = jnp.where(lane == 0, top, jnp.where(lane == 1, total, moment))
    a1[0] = jnp.transpose(packed)[0:4]

    def merge(ref, n):
        tops = [ref[k, 0:1, :] for k in range(n)]
        m = tops[0]
        for t in tops[1:]:
            m = jnp.maximum(m, t)
        s = jnp.zeros_like(m)
        q = jnp.zeros_like(m)
        for k in range(n):
            g = jnp.exp(tops[k] - m)
            s = s + g * ref[k, 1:2, :]
            q = q + g * ref[k, 2:3, :]
        return m, s, q

    def put(ref, rows):
        for i, r in enumerate(rows):
            ref[0, i:i + 1, :] = r

    def share(ref, ssems, rsems, moves):
        for k, where in moves:
            push(ref.at[0], ref.at[k], ssems.at[k], rsems.at[k], **where)
        for k, where in moves:
            got(ref.at[k], rsems.at[k])

    over_x = [(dx * NC + dc, dict(dx=dx, dc=dc)) for dx, dc in near]
    over_y = [(d, dict(dy=d)) for d in range(1, NY)]
    over_zh = [(d, dict(dzh=d)) for d in range(1, NZH)]
    over_z = [(d, dict(dz=d)) for d in range(1, nz)]
    share(a1, a1_s, a1_r, over_x)
    put(a2, merge(a1, NX * NC))
    share(a2, a2_s, a2_r, over_y)
    put(a3, merge(a2, NY))
    share(a3, a3_s, a3_r, over_zh)
    m, s, q = merge(a3, NZH)
    folds = jnp.where(zl == 0, fold[:, 0:th], fold[:, th:2 * th])
    keep = (folds != 0).astype(f32)
    row = lax.broadcasted_iota(jnp.int32, (128, th), 0)
    back = jnp.transpose(jnp.where(row == 0, m, jnp.where(row == 1, keep / s, q / s)))
    factor = jnp.exp(top - back[:, 0:1]) * back[:, 1:2]
    curving = (own[0] * factor * (own[1] - back[:, 2:3])).astype(bf16)
    cb[x, zl] = curving.reshape(2, qt, CW)

    ol = ls[1]
    xl, xr, xo = xs[-1], xs[1 % NX], xs[2 % NX]
    ahead, behind = dict(dx=1), dict(dx=NX - 1)

    def cpush(xx, ll, h, i, where):
        ref = cb.at[xx, ll, h]
        push(ref, ref, cx_s.at[i], cx_r.at[i], **where)

    def cgot(xx, ll, h, i):
        got(cb.at[xx, ll, h], cx_r.at[i])

    for h in range(2):
        me = cb.at[x, zl, h]
        push(me, me, cz_s.at[h], cz_r.at[h], dzl=1)
        if NX == 4:
            cpush(x, zl, h, h, ahead)
            cpush(x, zl, h, 2 + h, behind)
    got(cb.at[x, ol, 0], cz_r.at[0])
    if NX == 4:
        cpush(x, ol, 0, 4, ahead)
        cpush(x, ol, 0, 6, behind)
        cgot(xl, zl, 0, 0)
        cpush(xl, zl, 0, 8, ahead)
    got(cb.at[x, ol, 1], cz_r.at[1])
    if NX == 4:
        cpush(x, ol, 1, 7, behind)
        cgot(xr, zl, 1, 3)
        cpush(xr, zl, 1, 9, behind)
        cpush(x, ol, 1, 5, ahead)

    sums = [jnp.zeros((1, 128), f32) for _ in range(4)]
    img_moves = []

    def image(xb, sums):
        block = jnp.dot(ht[...], cb[xb].reshape(tok, CW), preferred_element_type=f32)
        d = dv[xb].reshape(F, CW).astype(f32)
        r = rv[xb].reshape(F, CW).astype(f32)
        g = block + DAMPING * d
        img[xb] = g
        img_moves.append(
            bring(
                img.at[xb], img_out.at[:, pl.ds(pl.multiple_of(xb * CW, 128), CW)],
                7 + 2 * NX + len(img_moves),
            )
        )
        terms = (r * r, r * g, g * g, d * g)
        rows = [jnp.sum(t, axis=0, keepdims=True) for t in terms]
        for i in range(0, CW, 128):
            sums = [a + t[:, i:i + 128] for a, t in zip(sums, rows)]
        return sums

    sums = image(x, sums)
    if NX == 4:
        cgot(xl, ol, 0, 4)
        cpush(xl, ol, 0, 10, ahead)
        cgot(xr, ol, 1, 7)
        cpush(xr, ol, 1, 11, behind)
        cgot(xl, zl, 1, 1)
        cgot(xl, ol, 1, 5)
        sums = image(xl, sums)
        cgot(xr, zl, 0, 2)
        cgot(xr, ol, 0, 6)
        sums = image(xr, sums)
        cgot(xo, zl, 0, 8)
        cgot(xo, zl, 1, 9)
        cgot(xo, ol, 0, 10)
        cgot(xo, ol, 1, 11)
        sums = image(xo, sums)

    def add(ref, n):
        s = ref[0]
        for k in range(1, n):
            s = s + ref[k]
        return s

    put(b1, sums)
    share(b1, b1_s, b1_r, over_x)
    b2[0] = add(b1, NX * NC)
    share(b2, b2_s, b2_r, over_y)
    b3[0] = add(b2, NY)
    share(b3, b3_s, b3_r, over_z)
    sums = jnp.sum(add(b3, nz), axis=1, keepdims=True)
    rr, ri, ii, di = sums[0:1], sums[1:2], sums[2:3], sums[3:4]
    step = rr / di
    mixing = (rr + step * (step * ii - 2.0 * ri)) / rr
    scal[0:1, :] = jnp.broadcast_to(step, (1, 128))
    scal[1:2, :] = jnp.broadcast_to(mixing, (1, 128))

    for d in img_moves:
        d.wait()
    for d in sends:
        d.wait_send()


def local(head_weight, direction, residual, hidden, fold_ids):
    f32, bf16 = jnp.float32, jnp.bfloat16
    hf = F // 2
    nb = NY * NZH
    tok = 16 * nb
    th = tok // 2
    vd = NX * CW
    vm, dma = pltpu.VMEM, pltpu.SemaphoreType.DMA
    anyspace = pl.BlockSpec(memory_space=pltpu.HBM)
    vspace = pl.BlockSpec(memory_space=pltpu.VMEM)

    def pair(*shape):
        return [dma(shape) if shape else dma, dma(shape) if shape else dma]

    scratch = [
        vm((1, tok), jnp.int32),
        vm((NX, NC, NZH, 8, hf), bf16),
        vm((NZH, 8, F), bf16),
        vm((NZH, 16, NX * hf), bf16),
        vm((nb, 16, 2 * NX * hf), bf16),
        vm((2, 2, NX, hf, CW), bf16),
        vm((NX, 2, hf, CW), bf16),
        vm((NX, 2, hf, CW), bf16),
        vm((NX, F, CW), f32),
        vm((NX, NZL, 2, th // 2, CW), bf16),
        vm((nb, 16, F), bf16),
        vm((F, tok), bf16),
        vm((2, th, CW), f32),
        vm((2, 2, th // 2, CW), jnp.int16),
        vm((2, 2, th // 2, CW), jnp.int16),
        vm((2, 2, 1, th // 2), f32),
        vm((2, 2, 1, th // 2), f32),
        vm((NX * NC, 4, th), f32),
        vm((NY, 4, th), f32),
        vm((NZH, 4, th), f32),
        vm((NX * NC, 4, 128), f32),
        vm((NY, 4, 128), f32),
        vm((NZH * NZL, 4, 128), f32),
        *pair(2, NX * NC), *pair(NZH), *pair(2, max(NY // 2, 1), NZH), *pair(NY, NZH),
        *pair(2, 2, NX), dma((7 + 3 * NX + NZH,)), *pair(2, 2), *pair(2, 2), *pair(2), *pair(12),
        *pair(NX * NC), *pair(NY), *pair(NZH),
        *pair(NX * NC), *pair(NY), *pair(NZH * NZL),
    ]
    image, scalars = pl.pallas_call(
        kernel,
        out_shape=(
            jax.ShapeDtypeStruct((F, vd), f32), jax.ShapeDtypeStruct((2, 128), f32)
        ),
        in_specs=[anyspace] * 5,
        out_specs=(anyspace, vspace),
        scratch_shapes=scratch,
        compiler_params=pltpu.CompilerParams(
            collective_id=0, has_side_effects=True, vmem_limit_bytes=67043328
        ),
    )(
        head_weight.reshape(2, hf, vd), direction.reshape(2, hf, vd),
        residual.reshape(2, hf, vd), hidden, fold_ids.reshape(1, tok),
    )
    moved = residual.astype(f32) - scalars[0:1, 0:1] * image
    return (moved + scalars[1:2, 0:1] * direction.astype(f32)).astype(bf16)


def solution(mesh):
    placed = (
        P("width", "vocab"),
        P("width", "vocab"),
        P("width", "vocab"),
        P("vocab", "width"),
        P(),
    )
    return jax.shard_map(
        local, mesh=mesh, in_specs=placed, out_specs=P("width", "vocab"), check_vma=False
    )
```

```python
import jax
import jax.numpy as jnp
from jax import lax
from jax.experimental import pallas as pl
from jax.experimental.pallas import tpu as pltpu
from jax.sharding import PartitionSpec as P

DAMPING = 0.02
MESH = pl.DeviceIdType.MESH
NY, NZH, NC, NZL, NX = 8, 4, 2, 2, 4
F = 512
CW = 256


def kernel(
    head, dirn, res, hid, fold_hbm, out,
    fold, hp, hz, hq, hg, wb, dv, rv, img, cb, hown, ht, own, zs, zr, us, ur,
    a1, a2, a3, b1, b2, b3,
    hx_s, hx_r, hz_s, hz_r, yr_s, yr_r, sb_s, sb_r,
    w_s, w_r, loc, z_s, z_r, u_s, u_r, cz_s, cz_r, cx_s, cx_r,
    a1_s, a1_r, a2_s, a2_r, a3_s, a3_r,
    b1_s, b1_r, b2_s, b2_r, b3_s, b3_r,
):
    f32, bf16 = jnp.float32, jnp.bfloat16
    hf = F // 2
    hl = NX * hf
    nb = NY * NZH
    nb2 = nb // 2
    tok = 16 * nb
    th = tok // 2
    qt = th // 2
    nz = NZH * NZL

    v = lax.axis_index("vocab")
    w = lax.axis_index("width")
    c = lax.rem(v, NC)
    zh = lax.rem(lax.div(v, NC), NZH)
    y = lax.div(v, NC * NZH)
    x = lax.rem(w, NX)
    zl = lax.div(w, NX)
    z = zh * NZL + zl

    xs = [x] + [lax.rem(x + d, NX) for d in range(1, NX)]
    ys = [y] + [lax.rem(y + d, NY) for d in range(1, NY)]
    hs = [zh] + [lax.rem(zh + d, NZH) for d in range(1, NZH)]
    cs = [c, 1 - c]
    ls = [zl, 1 - zl]
    zs_ = [z] + [lax.rem(z + d, nz) for d in range(1, nz)]
    vy = [i * (NZH * NC) for i in ys]
    vh = [i * NC for i in hs]
    wl = [i * NX for i in ls]

    def dev(dy=0, dzh=0, dc=0, dzl=0, dx=0, dz=0):
        if dz:
            hh = lax.div(zs_[dz], NZL)
            return (vy[dy] + hh * NC + cs[dc], (zs_[dz] - hh * NZL) * NX + xs[dx])
        return (vy[dy] + vh[dzh] + cs[dc], wl[dzl] + xs[dx])

    near = [(dx, dc) for dx in range(NX) for dc in range(NC) if dx or dc]
    peers = [dict(dx=dx, dc=dc) for dx, dc in near]
    peers += [dict(dy=d) for d in sorted({1, NY - 1})]
    peers += [dict(dzh=d) for d in range(1, NZH)]
    peers += [dict(dzl=1)]

    sends = []

    def push(src, dst, ssem, rsem, **where):
        d = pltpu.make_async_remote_copy(
            src_ref=src, dst_ref=dst, send_sem=ssem, recv_sem=rsem,
            device_id=dev(**where), device_id_type=MESH,
        )
        d.start()
        sends.append(d)

    def got(dst, rsem):
        pltpu.make_async_copy(dst, dst, rsem).wait()

    def bring(src, dst, i):
        d = pltpu.make_async_copy(src, dst, loc.at[i])
        d.start()
        return d

    barrier = pltpu.get_barrier_semaphore()
    for p in peers:
        pl.semaphore_signal(barrier, inc=1, device_id=dev(**p), device_id_type=MESH)
    own_hid = bring(hid, hz.at[0], 0)
    keeps = [bring(fold_hbm, fold, 1)]
    for xb in range(NX):
        keeps.append(bring(dirn.at[:, :, pl.ds(xb * CW, CW)], dv.at[xb], 2 + 2 * xb))
        keeps.append(bring(res.at[:, :, pl.ds(xb * CW, CW)], rv.at[xb], 3 + 2 * xb))
    own_w = {}
    arrays = (head, dirn)
    for arr in (1, 0):
        own_w[arr] = bring(
            arrays[arr].at[:, :, pl.ds(pl.multiple_of(x * CW, 128), CW)],
            wb.at[arr, :, x], 2 + 2 * NX + arr,
        )
    own_hid.wait()
    pl.semaphore_wait(barrier, len(peers))

    parts = [pl.multiple_of(i * hf, 128) for i in cs]
    for dx, dc in near:
        k = dx * NC + dc
        push(
            hz.at[0, :, pl.ds(parts[dc], hf)], hp.at[x, c, 0],
            hx_s.at[0, k], hx_r.at[0, k], dx=dx, dc=dc,
        )
    for d in range(1, NZH):
        push(hz.at[0], hz.at[d], hz_s.at[d], hz_r.at[d], dzh=d)

    def columns(arr, h):
        for dx in (1, 3, 2)[:NX - 1]:
            cols = pl.ds(pl.multiple_of(xs[dx] * CW, 128), CW)
            push(
                arrays[arr].at[h, :, cols], wb.at[arr, h, x],
                w_s.at[arr, h, dx], w_r.at[arr, h, dx], dx=dx,
            )

    columns(1, 0)
    own_piece = bring(hz.at[0, :, pl.ds(parts[0], hf)], hp.at[x, c, 0], 0)
    own_piece.wait()

    def slot(yy, zz, cc):
        return hg.at[yy * NZH + zz, :, pl.ds(pl.multiple_of(cc * hl, 128), hl)]

    def at(k, j, cc):
        return slot(ys[-k % NY], hs[-j % NZH], cc)

    def collect(first, n):
        for dx, dc in near:
            got(
                hp.at[xs[-dx % NX], cs[dc], pl.ds(first, n)],
                hx_r.at[min(first, 1), dx * NC + dc],
            )
        for j in range(first, first + n):
            for xb in range(NX):
                hq[j, :, xb * hf:(xb + 1) * hf] = jnp.concatenate(
                    [hp[xb, 0, j].astype(f32), hp[xb, 1, j].astype(f32)], axis=0
                ).astype(bf16)
            keeps.append(bring(hq.at[j], at(0, j, c), 7 + 3 * NX + j))

    last = {(0, j): NY // 2 - (0 if 2 * j <= NZH - 1 else 1) for j in range(NZH)}
    last.update({(1, j): NY - 1 - last[0, j] for j in range(NZH)})
    free = [0.0, 0.0]
    events = []

    def ring(src, k, j, way, s, now):
        if s < last[way, j]:
            dst = at(k, j, c)
            push(src, dst, yr_s.at[way, s, j], yr_r.at[way, s, j], dy=(1, NY - 1)[way])
            begin = max(now, free[way])
            free[way] = begin + 0.8
            events.append((begin + 2.4, len(events), way, s + 1, j))

    def arrive(src, k, j, ways, s, now):
        for way in ways:
            ring(src, k, j, way, s, now)
        push(src, at(k, j, c), sb_s.at[k, j], sb_r.at[k, j], dc=1)

    collect(0, 1)
    arrive(hq.at[0], 0, 0, (0, 1), 0, 0.0)
    for d in range(1, NZH):
        got(hz.at[d], hz_r.at[d])
    if NZH > 1:
        rest = pl.ds(1, NZH - 1)
        for dx, dc in near:
            k = dx * NC + dc
            push(
                hz.at[rest, :, pl.ds(parts[dc], hf)], hp.at[x, c, rest],
                hx_s.at[1, k], hx_r.at[1, k], dx=dx, dc=dc,
            )
        rest_copy = bring(hz.at[rest, :, pl.ds(parts[0], hf)], hp.at[x, c, rest], 4 + 2 * NX)
        events.append((4.5, len(events), 2, 0, 1))
    columns(1, 1)
    columns(0, 0)
    columns(0, 1)
    done = set()
    while len(done) < len(events):
        now, tag, way, s, j = min(e for e in events if e[1] not in done)
        done.add(tag)
        if way == 2:
            rest_copy.wait()
            collect(1, NZH - 1)
            for j in range(1, NZH):
                arrive(hq.at[j], 0, j, (0, 1), 0, now)
        else:
            k = s if way == 0 else NY - s
            got(at(k, j, c), yr_r.at[way, s - 1, j])
            arrive(at(k, j, c), k, j, (way,), s, now)
    for k in range(NY):
        for j in range(NZH):
            got(at(k, j, 1 - c), sb_r.at[k, j])
    for d in keeps:
        d.wait()

    for arr in (1, 0):
        for h in range(2):
            for dx in range(1, NX):
                got(wb.at[arr, h, xs[-dx % NX]], w_r.at[arr, h, dx])
        own_w[arr].wait()
        for h in range(2):
            rows = hg[pl.ds((1 - zl) * nb2 + h * (nb2 // 2), nb2 // 2)].reshape(qt, 2 * hl)
            part = jnp.dot(rows, wb[arr].reshape(2 * hl, CW), preferred_element_type=f32)
            reach = jnp.maximum(jnp.max(jnp.abs(part), axis=1, keepdims=True), 1e-30)
            steps = (part * (32767.0 / reach) + 32768.5).astype(jnp.int32) - 32768
            zs[arr, h] = steps.astype(jnp.int16)
            push(zs.at[arr, h], zr.at[arr, h], z_s.at[arr, h], z_r.at[arr, h], dzl=1)
            wide = jnp.broadcast_to(reach * (1.0 / 32767.0), (qt, 128))
            us[arr, h] = jnp.transpose(wide)[0:1]
            push(us.at[arr, h], ur.at[arr, h], u_s.at[arr, h], u_r.at[arr, h], dzl=1)
    for arr in (1, 0):
        rows = hg[pl.ds(zl * nb2, nb2)].reshape(th, 2 * hl)
        own[arr] = jnp.dot(rows, wb[arr].reshape(2 * hl, CW), preferred_element_type=f32)

    tails = [
        bring(
            hg.at[:, :, pl.ds(pl.multiple_of(h * hl + x * hf, 128), hf)],
            hown.at[:, :, pl.ds(h * hf, hf)], 5 + 2 * NX + h,
        )
        for h in range(2)
    ]
    for d in tails:
        d.wait()
    ht[...] = jnp.transpose(hown[...].reshape(tok, F).astype(f32)).astype(bf16)

    def whole(arr):
        parts = []
        for h in range(2):
            got(ur.at[arr, h], u_r.at[arr, h])
            unit = jnp.transpose(jnp.broadcast_to(ur[arr, h], (128, qt)))[:, 0:1]
            got(zr.at[arr, h], z_r.at[arr, h])
            parts.append(
                own[arr, h * qt:(h + 1) * qt] + zr[arr, h].astype(jnp.int32).astype(f32) * unit
            )
        return jnp.concatenate(parts, axis=0)

    squares = jnp.zeros((1, 128), f32)
    for xb in range(NX):
        r = rv[xb].reshape(F, CW).astype(f32)
        t = jnp.sum(r * r, axis=0, keepdims=True)
        for i in range(0, CW, 128):
            squares = squares + t[:, i:i + 128]
    tangent = whole(1)
    logits = whole(0)
    top = jnp.max(logits, axis=1, keepdims=True)
    e = jnp.exp(logits - top)
    total = jnp.sum(e, axis=1, keepdims=True)
    moment = jnp.sum(e * tangent, axis=1, keepdims=True)
    own[0] = e
    own[1] = tangent
    lane = lax.broadcasted_iota(jnp.int32, (th, 128), 1)
    packed = jnp.where(lane == 0, top, jnp.where(lane == 1, total, moment))
    a1[0] = jnp.transpose(packed)[0:4]

    def merge(ref, n):
        tops = [ref[k, 0:1, :] for k in range(n)]
        m = tops[0]
        for t in tops[1:]:
            m = jnp.maximum(m, t)
        s = jnp.zeros_like(m)
        q = jnp.zeros_like(m)
        for k in range(n):
            g = jnp.exp(tops[k] - m)
            s = s + g * ref[k, 1:2, :]
            q = q + g * ref[k, 2:3, :]
        return m, s, q

    def put(ref, rows):
        for i, r in enumerate(rows):
            ref[0, i:i + 1, :] = r

    def share(ref, ssems, rsems, moves):
        for k, where in moves:
            push(ref.at[0], ref.at[k], ssems.at[k], rsems.at[k], **where)
        for k, where in moves:
            got(ref.at[k], rsems.at[k])

    over_x = [(dx * NC + dc, dict(dx=dx, dc=dc)) for dx, dc in near]
    over_y = [(d, dict(dy=d)) for d in range(1, NY)]
    over_zh = [(d, dict(dzh=d)) for d in range(1, NZH)]
    over_z = [(d, dict(dz=d)) for d in range(1, nz)]
    share(a1, a1_s, a1_r, over_x)
    put(a2, merge(a1, NX * NC))
    share(a2, a2_s, a2_r, over_y)
    put(a3, merge(a2, NY))
    share(a3, a3_s, a3_r, over_zh)
    m, s, q = merge(a3, NZH)
    folds = jnp.where(zl == 0, fold[:, 0:th], fold[:, th:2 * th])
    keep = (folds != 0).astype(f32)
    row = lax.broadcasted_iota(jnp.int32, (128, th), 0)
    back = jnp.transpose(jnp.where(row == 0, m, jnp.where(row == 1, keep / s, q / s)))
    factor = jnp.exp(top - back[:, 0:1]) * back[:, 1:2]
    curving = (own[0] * factor * (own[1] - back[:, 2:3])).astype(bf16)
    cb[x, zl] = curving.reshape(2, qt, CW)

    ol = ls[1]
    xl, xr, xo = xs[-1], xs[1 % NX], xs[2 % NX]
    ahead, behind = dict(dx=1), dict(dx=NX - 1)

    def cpush(xx, ll, h, i, where):
        ref = cb.at[xx, ll, h]
        push(ref, ref, cx_s.at[i], cx_r.at[i], **where)

    def cgot(xx, ll, h, i):
        got(cb.at[xx, ll, h], cx_r.at[i])

    for h in range(2):
        me = cb.at[x, zl, h]
        push(me, me, cz_s.at[h], cz_r.at[h], dzl=1)
        if NX == 4:
            cpush(x, zl, h, h, ahead)
            cpush(x, zl, h, 2 + h, behind)
    got(cb.at[x, ol, 0], cz_r.at[0])
    if NX == 4:
        cpush(x, ol, 0, 4, ahead)
        cpush(x, ol, 0, 6, behind)
        cgot(xl, zl, 0, 0)
        cpush(xl, zl, 0, 8, ahead)
    got(cb.at[x, ol, 1], cz_r.at[1])
    if NX == 4:
        cpush(x, ol, 1, 7, behind)
        cgot(xr, zl, 1, 3)
        cpush(xr, zl, 1, 9, behind)
        cpush(x, ol, 1, 5, ahead)

    sums = [jnp.zeros((1, 128), f32) for _ in range(3)]

    def image(xb, sums):
        block = jnp.dot(ht[...], cb[xb].reshape(tok, CW), preferred_element_type=f32)
        d = dv[xb].reshape(F, CW).astype(f32)
        r = rv[xb].reshape(F, CW).astype(f32)
        g = block + DAMPING * d
        img[xb] = g
        terms = (r * g, g * g, d * g)
        rows = [jnp.sum(t, axis=0, keepdims=True) for t in terms]
        for i in range(0, CW, 128):
            sums = [a + t[:, i:i + 128] for a, t in zip(sums, rows)]
        return sums

    sums = image(x, sums)
    if NX == 4:
        cgot(xl, ol, 0, 4)
        cpush(xl, ol, 0, 10, ahead)
        cgot(xr, ol, 1, 7)
        cpush(xr, ol, 1, 11, behind)
        cgot(xl, zl, 1, 1)
        cgot(xl, ol, 1, 5)
        sums = image(xl, sums)
        cgot(xr, zl, 0, 2)
        cgot(xr, ol, 0, 6)
        sums = image(xr, sums)
        cgot(xo, zl, 0, 8)
        cgot(xo, zl, 1, 9)
        cgot(xo, ol, 0, 10)
        cgot(xo, ol, 1, 11)
        sums = image(xo, sums)

    def add(ref, n):
        s = ref[0]
        for k in range(1, n):
            s = s + ref[k]
        return s

    put(b1, [squares] + sums)
    share(b1, b1_s, b1_r, over_x)
    b2[0] = add(b1, NX * NC)
    share(b2, b2_s, b2_r, over_y)
    b3[0] = add(b2, NY)
    share(b3, b3_s, b3_r, over_z)
    sums = jnp.sum(add(b3, nz), axis=1, keepdims=True)
    rr, ri, ii, di = sums[0:1], sums[1:2], sums[2:3], sums[3:4]
    step = rr / di
    mixing = (rr + step * (step * ii - 2.0 * ri)) / rr
    for xb in range(NX):
        d = dv[xb].reshape(F, CW).astype(f32)
        r = rv[xb].reshape(F, CW).astype(f32)
        out[:, xb * CW:(xb + 1) * CW] = ((r - step * img[xb]) + mixing * d).astype(bf16)

    for d in sends:
        d.wait_send()


def local(head_weight, direction, residual, hidden, fold_ids):
    f32, bf16 = jnp.float32, jnp.bfloat16
    hf = F // 2
    nb = NY * NZH
    tok = 16 * nb
    th = tok // 2
    vd = NX * CW
    vm, dma = pltpu.VMEM, pltpu.SemaphoreType.DMA
    anyspace = pl.BlockSpec(memory_space=pltpu.HBM)
    vspace = pl.BlockSpec(memory_space=pltpu.VMEM)

    def pair(*shape):
        return [dma(shape) if shape else dma, dma(shape) if shape else dma]

    scratch = [
        vm((1, tok), jnp.int32),
        vm((NX, NC, NZH, 8, hf), bf16),
        vm((NZH, 8, F), bf16),
        vm((NZH, 16, NX * hf), bf16),
        vm((nb, 16, 2 * NX * hf), bf16),
        vm((2, 2, NX, hf, CW), bf16),
        vm((NX, 2, hf, CW), bf16),
        vm((NX, 2, hf, CW), bf16),
        vm((NX, F, CW), f32),
        vm((NX, NZL, 2, th // 2, CW), bf16),
        vm((nb, 16, F), bf16),
        vm((F, tok), bf16),
        vm((2, th, CW), f32),
        vm((2, 2, th // 2, CW), jnp.int16),
        vm((2, 2, th // 2, CW), jnp.int16),
        vm((2, 2, 1, th // 2), f32),
        vm((2, 2, 1, th // 2), f32),
        vm((NX * NC, 4, th), f32),
        vm((NY, 4, th), f32),
        vm((NZH, 4, th), f32),
        vm((NX * NC, 4, 128), f32),
        vm((NY, 4, 128), f32),
        vm((NZH * NZL, 4, 128), f32),
        *pair(2, NX * NC), *pair(NZH), *pair(2, max(NY // 2, 1), NZH), *pair(NY, NZH),
        *pair(2, 2, NX), dma((7 + 3 * NX + NZH,)), *pair(2, 2), *pair(2, 2), *pair(2), *pair(12),
        *pair(NX * NC), *pair(NY), *pair(NZH),
        *pair(NX * NC), *pair(NY), *pair(NZH * NZL),
    ]
    return pl.pallas_call(
        kernel,
        out_shape=jax.ShapeDtypeStruct((F, vd), bf16),
        in_specs=[anyspace] * 5,
        out_specs=vspace,
        scratch_shapes=scratch,
        compiler_params=pltpu.CompilerParams(
            collective_id=0, has_side_effects=True, vmem_limit_bytes=67043328
        ),
    )(
        head_weight.reshape(2, hf, vd), direction.reshape(2, hf, vd),
        residual.reshape(2, hf, vd), hidden, fold_ids.reshape(1, tok),
    )


def solution(mesh):
    placed = (
        P("width", "vocab"),
        P("width", "vocab"),
        P("width", "vocab"),
        P("vocab", "width"),
        P(),
    )
    return jax.shard_map(
        local, mesh=mesh, in_specs=placed, out_specs=P("width", "vocab"), check_vma=False
    )
```

```python
import jax
import jax.numpy as jnp
from jax import lax
from jax.experimental import pallas as pl
from jax.experimental.pallas import tpu as pltpu
from jax.sharding import PartitionSpec as P

DAMPING = 0.02
MESH = pl.DeviceIdType.MESH
NY, NZH, NC, NZL, NX = 8, 4, 2, 2, 4
F = 512
CW = 256


def kernel(
    head, dirn, res, hid, fold_hbm, out,
    fold, hp, hz, hq, hg, wb, dv, rv, img, cb, hown, ht, own, zs, zr, us, ur,
    a1, a2, a3, b1, b2, b3,
    hx_s, hx_r, hz_s, hz_r, yr_s, yr_r, sb_s, sb_r,
    w_s, w_r, loc, z_s, z_r, u_s, u_r, cz_s, cz_r, cx_s, cx_r,
    a1_s, a1_r, a2_s, a2_r, a3_s, a3_r,
    b1_s, b1_r, b2_s, b2_r, b3_s, b3_r,
):
    f32, bf16 = jnp.float32, jnp.bfloat16
    hf = F // 2
    hl = NX * hf
    nb = NY * NZH
    nb2 = nb // 2
    tok = 16 * nb
    th = tok // 2
    qt = th // 2
    nz = NZH * NZL

    v = lax.axis_index("vocab")
    w = lax.axis_index("width")
    c = lax.rem(v, NC)
    zh = lax.rem(lax.div(v, NC), NZH)
    y = lax.div(v, NC * NZH)
    x = lax.rem(w, NX)
    zl = lax.div(w, NX)
    z = zh * NZL + zl

    xs = [x] + [lax.rem(x + d, NX) for d in range(1, NX)]
    ys = [y] + [lax.rem(y + d, NY) for d in range(1, NY)]
    hs = [zh] + [lax.rem(zh + d, NZH) for d in range(1, NZH)]
    cs = [c, 1 - c]
    ls = [zl, 1 - zl]
    zs_ = [z] + [lax.rem(z + d, nz) for d in range(1, nz)]
    vy = [i * (NZH * NC) for i in ys]
    vh = [i * NC for i in hs]
    wl = [i * NX for i in ls]

    def dev(dy=0, dzh=0, dc=0, dzl=0, dx=0, dz=0):
        if dz:
            hh = lax.div(zs_[dz], NZL)
            return (vy[dy] + hh * NC + cs[dc], (zs_[dz] - hh * NZL) * NX + xs[dx])
        return (vy[dy] + vh[dzh] + cs[dc], wl[dzl] + xs[dx])

    near = [(dx, dc) for dx in range(NX) for dc in range(NC) if dx or dc]
    peers = [dict(dx=dx, dc=dc) for dx, dc in near]
    peers += [dict(dy=d) for d in sorted({1, NY - 1})]
    peers += [dict(dzh=d) for d in range(1, NZH)]
    peers += [dict(dzl=1)]

    sends = []

    def push(src, dst, ssem, rsem, **where):
        d = pltpu.make_async_remote_copy(
            src_ref=src, dst_ref=dst, send_sem=ssem, recv_sem=rsem,
            device_id=dev(**where), device_id_type=MESH,
        )
        d.start()
        sends.append(d)

    def got(dst, rsem):
        pltpu.make_async_copy(dst, dst, rsem).wait()

    def bring(src, dst, i):
        d = pltpu.make_async_copy(src, dst, loc.at[i])
        d.start()
        return d

    barrier = pltpu.get_barrier_semaphore()
    for p in peers:
        pl.semaphore_signal(barrier, inc=1, device_id=dev(**p), device_id_type=MESH)
    own_hid = bring(hid, hz.at[0], 0)
    keeps = [bring(fold_hbm, fold, 1)]
    for xb in range(NX):
        keeps.append(bring(dirn.at[:, :, pl.ds(xb * CW, CW)], dv.at[xb], 2 + 2 * xb))
        keeps.append(bring(res.at[:, :, pl.ds(xb * CW, CW)], rv.at[xb], 3 + 2 * xb))
    own_w = {}
    arrays = (head, dirn)
    for arr in (1, 0):
        own_w[arr] = bring(
            arrays[arr].at[:, :, pl.ds(pl.multiple_of(x * CW, 128), CW)],
            wb.at[arr, :, x], 2 + 2 * NX + arr,
        )
    own_hid.wait()
    pl.semaphore_wait(barrier, len(peers))

    parts = [pl.multiple_of(i * hf, 128) for i in cs]
    for dx, dc in near:
        k = dx * NC + dc
        push(
            hz.at[0, :, pl.ds(parts[dc], hf)], hp.at[x, c, 0],
            hx_s.at[0, k], hx_r.at[0, k], dx=dx, dc=dc,
        )
    for d in range(1, NZH):
        push(hz.at[0], hz.at[d], hz_s.at[d], hz_r.at[d], dzh=d)

    def columns(arr, h, ways=(1, 3, 2)):
        for dx in ways[:NX - 1]:
            cols = pl.ds(pl.multiple_of(xs[dx] * CW, 128), CW)
            push(
                arrays[arr].at[h, :, cols], wb.at[arr, h, x],
                w_s.at[arr, h, dx], w_r.at[arr, h, dx], dx=dx,
            )

    columns(1, 0, (1, 3))
    own_piece = bring(hz.at[0, :, pl.ds(parts[0], hf)], hp.at[x, c, 0], 0)
    own_piece.wait()

    def slot(yy, zz, cc):
        return hg.at[yy * NZH + zz, :, pl.ds(pl.multiple_of(cc * hl, 128), hl)]

    def at(k, j, cc):
        return slot(ys[-k % NY], hs[-j % NZH], cc)

    def collect(first, n):
        for dx, dc in near:
            got(
                hp.at[xs[-dx % NX], cs[dc], pl.ds(first, n)],
                hx_r.at[min(first, 1), dx * NC + dc],
            )
        for j in range(first, first + n):
            for xb in range(NX):
                hq[j, :, xb * hf:(xb + 1) * hf] = jnp.concatenate(
                    [hp[xb, 0, j].astype(f32), hp[xb, 1, j].astype(f32)], axis=0
                ).astype(bf16)
            keeps.append(bring(hq.at[j], at(0, j, c), 7 + 3 * NX + j))

    last = {(0, j): NY // 2 - (0 if 2 * j <= NZH - 1 else 1) for j in range(NZH)}
    last.update({(1, j): NY - 1 - last[0, j] for j in range(NZH)})
    free = [0.0, 0.0]
    events = []

    def ring(src, k, j, way, s, now):
        if s < last[way, j]:
            dst = at(k, j, c)
            push(src, dst, yr_s.at[way, s, j], yr_r.at[way, s, j], dy=(1, NY - 1)[way])
            begin = max(now, free[way])
            free[way] = begin + 0.8
            events.append((begin + 2.4, len(events), way, s + 1, j))

    def arrive(src, k, j, ways, s, now):
        for way in ways:
            ring(src, k, j, way, s, now)
        push(src, at(k, j, c), sb_s.at[k, j], sb_r.at[k, j], dc=1)

    collect(0, 1)
    arrive(hq.at[0], 0, 0, (0, 1), 0, 0.0)
    for d in range(1, NZH):
        got(hz.at[d], hz_r.at[d])
    if NZH > 1:
        rest = pl.ds(1, NZH - 1)
        for dx, dc in near:
            k = dx * NC + dc
            push(
                hz.at[rest, :, pl.ds(parts[dc], hf)], hp.at[x, c, rest],
                hx_s.at[1, k], hx_r.at[1, k], dx=dx, dc=dc,
            )
        rest_copy = bring(hz.at[rest, :, pl.ds(parts[0], hf)], hp.at[x, c, rest], 4 + 2 * NX)
        events.append((4.5, len(events), 2, 0, 1))
    columns(1, 0, (2,))
    columns(1, 1)
    columns(0, 0)
    columns(0, 1)
    done = set()
    while len(done) < len(events):
        now, tag, way, s, j = min(e for e in events if e[1] not in done)
        done.add(tag)
        if way == 2:
            rest_copy.wait()
            collect(1, NZH - 1)
            for j in range(1, NZH):
                arrive(hq.at[j], 0, j, (0, 1), 0, now)
        else:
            k = s if way == 0 else NY - s
            got(at(k, j, c), yr_r.at[way, s - 1, j])
            arrive(at(k, j, c), k, j, (way,), s, now)
    for k in range(NY):
        for j in range(NZH):
            got(at(k, j, 1 - c), sb_r.at[k, j])
    for d in keeps:
        d.wait()

    for arr in (1, 0):
        for h in range(2):
            for dx in range(1, NX):
                got(wb.at[arr, h, xs[-dx % NX]], w_r.at[arr, h, dx])
        own_w[arr].wait()
        for h in range(2):
            rows = hg[pl.ds((1 - zl) * nb2 + h * (nb2 // 2), nb2 // 2)].reshape(qt, 2 * hl)
            part = jnp.dot(rows, wb[arr].reshape(2 * hl, CW), preferred_element_type=f32)
            reach = jnp.maximum(jnp.max(jnp.abs(part), axis=1, keepdims=True), 1e-30)
            steps = (part * (32767.0 / reach) + 32768.5).astype(jnp.int32) - 32768
            zs[arr, h] = steps.astype(jnp.int16)
            push(zs.at[arr, h], zr.at[arr, h], z_s.at[arr, h], z_r.at[arr, h], dzl=1)
            wide = jnp.broadcast_to(reach * (1.0 / 32767.0), (qt, 128))
            us[arr, h] = jnp.transpose(wide)[0:1]
            push(us.at[arr, h], ur.at[arr, h], u_s.at[arr, h], u_r.at[arr, h], dzl=1)
    for arr in (1, 0):
        rows = hg[pl.ds(zl * nb2, nb2)].reshape(th, 2 * hl)
        own[arr] = jnp.dot(rows, wb[arr].reshape(2 * hl, CW), preferred_element_type=f32)

    tails = [
        bring(
            hg.at[:, :, pl.ds(pl.multiple_of(h * hl + x * hf, 128), hf)],
            hown.at[:, :, pl.ds(h * hf, hf)], 5 + 2 * NX + h,
        )
        for h in range(2)
    ]
    for d in tails:
        d.wait()
    ht[...] = jnp.transpose(hown[...].reshape(tok, F).astype(f32)).astype(bf16)

    def whole(arr):
        parts = []
        for h in range(2):
            got(ur.at[arr, h], u_r.at[arr, h])
            unit = jnp.transpose(jnp.broadcast_to(ur[arr, h], (128, qt)))[:, 0:1]
            got(zr.at[arr, h], z_r.at[arr, h])
            parts.append(
                own[arr, h * qt:(h + 1) * qt] + zr[arr, h].astype(jnp.int32).astype(f32) * unit
            )
        return jnp.concatenate(parts, axis=0)

    squares = jnp.zeros((1, 128), f32)
    for xb in range(NX):
        r = rv[xb].reshape(F, CW).astype(f32)
        t = jnp.sum(r * r, axis=0, keepdims=True)
        for i in range(0, CW, 128):
            squares = squares + t[:, i:i + 128]
    tangent = whole(1)
    logits = whole(0)
    top = jnp.max(logits, axis=1, keepdims=True)
    e = jnp.exp(logits - top)
    total = jnp.sum(e, axis=1, keepdims=True)
    moment = jnp.sum(e * tangent, axis=1, keepdims=True)
    own[0] = e
    own[1] = tangent
    lane = lax.broadcasted_iota(jnp.int32, (th, 128), 1)
    packed = jnp.where(lane == 0, top, jnp.where(lane == 1, total, moment))
    a1[0] = jnp.transpose(packed)[0:4]

    def merge(ref, n):
        tops = [ref[k, 0:1, :] for k in range(n)]
        m = tops[0]
        for t in tops[1:]:
            m = jnp.maximum(m, t)
        s = jnp.zeros_like(m)
        q = jnp.zeros_like(m)
        for k in range(n):
            g = jnp.exp(tops[k] - m)
            s = s + g * ref[k, 1:2, :]
            q = q + g * ref[k, 2:3, :]
        return m, s, q

    def put(ref, rows):
        for i, r in enumerate(rows):
            ref[0, i:i + 1, :] = r

    def share(ref, ssems, rsems, moves):
        for k, where in moves:
            push(ref.at[0], ref.at[k], ssems.at[k], rsems.at[k], **where)
        for k, where in moves:
            got(ref.at[k], rsems.at[k])

    over_x = [(dx * NC + dc, dict(dx=dx, dc=dc)) for dx, dc in near]
    over_y = [(d, dict(dy=d)) for d in range(1, NY)]
    over_zh = [(d, dict(dzh=d)) for d in range(1, NZH)]
    over_z = [(d, dict(dz=d)) for d in range(1, nz)]
    share(a1, a1_s, a1_r, over_x)
    put(a2, merge(a1, NX * NC))
    share(a2, a2_s, a2_r, over_y)
    put(a3, merge(a2, NY))
    share(a3, a3_s, a3_r, over_zh)
    m, s, q = merge(a3, NZH)
    folds = jnp.where(zl == 0, fold[:, 0:th], fold[:, th:2 * th])
    keep = (folds != 0).astype(f32)
    row = lax.broadcasted_iota(jnp.int32, (128, th), 0)
    back = jnp.transpose(jnp.where(row == 0, m, jnp.where(row == 1, keep / s, q / s)))
    factor = jnp.exp(top - back[:, 0:1]) * back[:, 1:2]
    curving = (own[0] * factor * (own[1] - back[:, 2:3])).astype(bf16)
    cb[x, zl] = curving.reshape(2, qt, CW)

    ol = ls[1]
    xl, xr, xo = xs[-1], xs[1 % NX], xs[2 % NX]
    ahead, behind = dict(dx=1), dict(dx=NX - 1)

    def cpush(xx, ll, h, i, where):
        ref = cb.at[xx, ll, h]
        push(ref, ref, cx_s.at[i], cx_r.at[i], **where)

    def cgot(xx, ll, h, i):
        got(cb.at[xx, ll, h], cx_r.at[i])

    for h in range(2):
        me = cb.at[x, zl, h]
        push(me, me, cz_s.at[h], cz_r.at[h], dzl=1)
        if NX == 4:
            cpush(x, zl, h, h, ahead)
            cpush(x, zl, h, 2 + h, behind)
    got(cb.at[x, ol, 0], cz_r.at[0])
    if NX == 4:
        cpush(x, ol, 0, 4, ahead)
        cpush(x, ol, 0, 6, behind)
        cgot(xl, zl, 0, 0)
        cpush(xl, zl, 0, 8, ahead)
    got(cb.at[x, ol, 1], cz_r.at[1])
    if NX == 4:
        cpush(x, ol, 1, 7, behind)
        cgot(xr, zl, 1, 3)
        cpush(xr, zl, 1, 9, behind)
        cpush(x, ol, 1, 5, ahead)

    sums = [jnp.zeros((1, 128), f32) for _ in range(3)]

    def image(xb, sums):
        block = jnp.dot(ht[...], cb[xb].reshape(tok, CW), preferred_element_type=f32)
        d = dv[xb].reshape(F, CW).astype(f32)
        r = rv[xb].reshape(F, CW).astype(f32)
        g = block + DAMPING * d
        img[xb] = g
        terms = (r * g, g * g, d * g)
        rows = [jnp.sum(t, axis=0, keepdims=True) for t in terms]
        for i in range(0, CW, 128):
            sums = [a + t[:, i:i + 128] for a, t in zip(sums, rows)]
        return sums

    sums = image(x, sums)
    if NX == 4:
        cgot(xl, ol, 0, 4)
        cpush(xl, ol, 0, 10, ahead)
        cgot(xr, ol, 1, 7)
        cpush(xr, ol, 1, 11, behind)
        cgot(xl, zl, 1, 1)
        cgot(xl, ol, 1, 5)
        sums = image(xl, sums)
        cgot(xr, zl, 0, 2)
        cgot(xr, ol, 0, 6)
        sums = image(xr, sums)
        cgot(xo, zl, 0, 8)
        cgot(xo, zl, 1, 9)
        cgot(xo, ol, 0, 10)
        cgot(xo, ol, 1, 11)
        sums = image(xo, sums)

    def add(ref, n):
        s = ref[0]
        for k in range(1, n):
            s = s + ref[k]
        return s

    put(b1, [squares] + sums)
    share(b1, b1_s, b1_r, over_x)
    b2[0] = add(b1, NX * NC)
    share(b2, b2_s, b2_r, over_y)
    b3[0] = add(b2, NY)
    share(b3, b3_s, b3_r, over_z)
    sums = jnp.sum(add(b3, nz), axis=1, keepdims=True)
    rr, ri, ii, di = sums[0:1], sums[1:2], sums[2:3], sums[3:4]
    step = rr / di
    mixing = (rr + step * (step * ii - 2.0 * ri)) / rr
    for xb in range(NX):
        d = dv[xb].reshape(F, CW).astype(f32)
        r = rv[xb].reshape(F, CW).astype(f32)
        out[:, xb * CW:(xb + 1) * CW] = ((r - step * img[xb]) + mixing * d).astype(bf16)

    for d in sends:
        d.wait_send()


def local(head_weight, direction, residual, hidden, fold_ids):
    f32, bf16 = jnp.float32, jnp.bfloat16
    hf = F // 2
    nb = NY * NZH
    tok = 16 * nb
    th = tok // 2
    vd = NX * CW
    vm, dma = pltpu.VMEM, pltpu.SemaphoreType.DMA
    anyspace = pl.BlockSpec(memory_space=pltpu.HBM)
    vspace = pl.BlockSpec(memory_space=pltpu.VMEM)

    def pair(*shape):
        return [dma(shape) if shape else dma, dma(shape) if shape else dma]

    scratch = [
        vm((1, tok), jnp.int32),
        vm((NX, NC, NZH, 8, hf), bf16),
        vm((NZH, 8, F), bf16),
        vm((NZH, 16, NX * hf), bf16),
        vm((nb, 16, 2 * NX * hf), bf16),
        vm((2, 2, NX, hf, CW), bf16),
        vm((NX, 2, hf, CW), bf16),
        vm((NX, 2, hf, CW), bf16),
        vm((NX, F, CW), f32),
        vm((NX, NZL, 2, th // 2, CW), bf16),
        vm((nb, 16, F), bf16),
        vm((F, tok), bf16),
        vm((2, th, CW), f32),
        vm((2, 2, th // 2, CW), jnp.int16),
        vm((2, 2, th // 2, CW), jnp.int16),
        vm((2, 2, 1, th // 2), f32),
        vm((2, 2, 1, th // 2), f32),
        vm((NX * NC, 4, th), f32),
        vm((NY, 4, th), f32),
        vm((NZH, 4, th), f32),
        vm((NX * NC, 4, 128), f32),
        vm((NY, 4, 128), f32),
        vm((NZH * NZL, 4, 128), f32),
        *pair(2, NX * NC), *pair(NZH), *pair(2, max(NY // 2, 1), NZH), *pair(NY, NZH),
        *pair(2, 2, NX), dma((7 + 3 * NX + NZH,)), *pair(2, 2), *pair(2, 2), *pair(2), *pair(12),
        *pair(NX * NC), *pair(NY), *pair(NZH),
        *pair(NX * NC), *pair(NY), *pair(NZH * NZL),
    ]
    return pl.pallas_call(
        kernel,
        out_shape=jax.ShapeDtypeStruct((F, vd), bf16),
        in_specs=[anyspace] * 5,
        out_specs=vspace,
        scratch_shapes=scratch,
        compiler_params=pltpu.CompilerParams(
            collective_id=0, has_side_effects=True, vmem_limit_bytes=67043328
        ),
    )(
        head_weight.reshape(2, hf, vd), direction.reshape(2, hf, vd),
        residual.reshape(2, hf, vd), hidden, fold_ids.reshape(1, tok),
    )


def solution(mesh):
    placed = (
        P("width", "vocab"),
        P("width", "vocab"),
        P("width", "vocab"),
        P("vocab", "width"),
        P(),
    )
    return jax.shard_map(
        local, mesh=mesh, in_specs=placed, out_specs=P("width", "vocab"), check_vma=False
    )
```
